256 devices in a mesh: row: 8 (over y, z_hi), col: 32 (over z_lo, x, core).
Axes of the slice: x: 4, y: 4, z: 8 (z_hi: 2, z_lo: 4; z = z_hi * 4 + z_lo), core: 2. Of those that a mesh axis runs over, the one named last changes fastest.
Arguments:
- transfer: bfloat16 [2, 4096, 16384], P(None, 'row', 'col'), may hold values from -0.046875 to 0.046875
- phase: float32 [16384, 128], P('col', 'row'), may hold values from -3.140625 to 3.140625
- trap_index: int32 [128, 64], replicated, may hold values from 0 to 4095
- levels: int32 [128, 64], replicated, may hold values from 1 to 4
- weights_old: float32 [128, 64], replicated, may hold values from 0.5 to 1.5
Outputs:
- far_field: bfloat16 [4096, 2, 128], P(('row', 'col'))
- weights_new: float32 [128, 64], replicated
- slm_field: float32 [16384, 2, 128], P('col', None, 'row')
The draws below stay inside these ranges and needn't reach their ends.
All inputs are finite; a program needn't handle non-finite values.
Results may differ from the reference program's by a relative error of at most 0.013.
Values may be sent and summed in bfloat16 or wider, within the bound.
A program may use at most 64 MiB of HBM per device.

```python
import jax
import jax.numpy as jnp
from jax import lax

MODES = 16384
PATTERNS = 128
TRAPS = 64
M = 4096


def place_ends(array, stream_key, smallest, top_value):
    shape = array.shape
    spot = [jax.random.randint(jax.random.fold_in(stream_key, axis), (), 0, shape[axis]) for axis in range(len(shape))]
    array = array.at[tuple(spot)].set(smallest)
    longest = shape.index(max(shape))
    spot[longest] = (spot[longest] + 1) % shape[longest]
    return array.at[tuple(spot)].set(top_value)


def level_of(stream_key, shape, pieces, least, high):
    level = 1.0
    for position, blocks in pieces:
        steps = jax.random.uniform(jax.random.fold_in(jax.random.fold_in(stream_key, 6), position), (blocks,), jnp.float32, least / len(pieces), high / len(pieces))
        level = level * jnp.repeat(jnp.exp(steps), shape[position] // blocks).reshape((-1,) + (1,) * (len(shape) - 1 - position))
    return level


def scatter_about(own_key, extent, width, limit, split=(), kind=jnp.bfloat16):
    drawn = width * jax.random.normal(own_key, extent, jnp.float32)
    if split:
        drawn = drawn * level_of(own_key, extent, split, -0.22, 0.18)
    return jnp.clip(drawn, -limit, limit).astype(kind)


def setup_inputs(seed: int = 0) -> dict:
    key_of = jax.random.split(jax.random.key(seed), 6)
    transfer = scatter_about(key_of[0], (2, M, MODES), MODES ** -0.5, 0.046875, ((1, 8), (2, 32)))
    phase = jnp.clip(jax.random.uniform(key_of[1], (MODES, PATTERNS), jnp.float32, -3.140625, 3.140625), -3.140625, 3.140625)
    trap_index = place_ends(jax.random.randint(key_of[2], (PATTERNS, TRAPS), 0, M), jax.random.fold_in(key_of[2], 1), 0, M - 1).astype(jnp.int32)
    levels = place_ends(jax.random.randint(key_of[3], (PATTERNS, TRAPS), 1, 5), jax.random.fold_in(key_of[3], 1), 1, 4).astype(jnp.int32)
    weights_old = jnp.clip(1.0 + 0.1 * jax.random.normal(key_of[4], (PATTERNS, TRAPS), jnp.float32), 0.5, 1.5)
    return {"transfer": transfer, "phase": phase, "trap_index": trap_index, "levels": levels, "weights_old": weights_old}


def reference(transfer, phase, trap_index, levels, weights_old):
    count = phase.shape[1]
    field_re = jnp.cos(phase).astype(jnp.bfloat16)
    field_im = jnp.sin(phase).astype(jnp.bfloat16)
    joined = jnp.concatenate([field_re, field_im], axis=1)
    first = jnp.dot(transfer[0], joined, preferred_element_type=jnp.float32)
    second = jnp.dot(transfer[1], joined, preferred_element_type=jnp.float32)
    out = jnp.stack([first[:, :count] - second[:, count:], first[:, count:] + second[:, :count]], axis=1)
    far_field = out.astype(jnp.bfloat16)
    pattern_ids = jnp.arange(count, dtype=jnp.int32)[:, None]
    values = out[trap_index, :, pattern_ids]
    amp = jnp.sqrt(values[..., 0] ** 2 + values[..., 1] ** 2 + 0.25)
    target = levels.astype(jnp.float32)
    ratio = amp / target
    mean_ratio = lax.optimization_barrier(jnp.mean(ratio, axis=1, keepdims=True))
    weights_new = weights_old * mean_ratio / ratio
    coef = weights_new * target / amp
    projected = jnp.zeros(out.shape, jnp.float32).at[trap_index, :, pattern_ids].add(coef[..., None] * values)
    projected = projected.astype(jnp.bfloat16)
    stacked = jnp.concatenate([projected[:, 0], projected[:, 1]], axis=1)
    dims = (((0,), (0,)), ((), ()))
    first_b = lax.dot_general(transfer[0], stacked, dims, preferred_element_type=jnp.float32)
    second_b = lax.dot_general(transfer[1], stacked, dims, preferred_element_type=jnp.float32)
    back = jnp.stack([first_b[:, :count] + second_b[:, count:], first_b[:, count:] - second_b[:, :count]], axis=1)
    scaled = jnp.sqrt(jnp.float32(MODES) / jnp.float32(TRAPS)) * back
    slm_field = scaled / jnp.sqrt(scaled[:, 0:1] ** 2 + scaled[:, 1:2] ** 2 + 1.0)
    return (far_field, weights_new, slm_field)
```

```python
import functools

import jax
import jax.numpy as jnp
from jax import lax
from jax.experimental import pallas as pl
from jax.experimental.pallas import tpu as pltpu
from jax.sharding import PartitionSpec as P

MODES = 16384
TRAPS = 64
MESH = pl.DeviceIdType.MESH
CHUNKS = 4


def kernel(
    n_row,
    n_col,
    scale,
    transfer_hbm,
    phase_hbm,
    trap_hbm,
    levels_hbm,
    old_hbm,
    far_ref,
    weights_ref,
    slm_ref,
    transfer,
    phase,
    trap,
    levels,
    old,
    fields,
    part,
    rs_buf,
    out_all,
    power,
    amp_pix,
    stage,
    back_buf,
    amp_rows,
    amp_buf,
    in_sem,
    field_send,
    field_recv,
    rs_send,
    rs_recv,
    ag_send,
    ag_recv,
    back_send,
    back_recv,
    amp_send,
    amp_recv,
):
    row = lax.axis_index("row")
    col = lax.axis_index("col")
    pix_rows = part.shape[1]
    patterns = part.shape[2] // 2
    tile_rows = transfer.shape[1]
    own = phase.shape[0]
    traps = trap.shape[0]
    group = n_col // CHUNKS

    barrier = pltpu.get_barrier_semaphore()

    def greet_row(step, carry):
        peer = lax.rem(row + step, n_row)
        pl.semaphore_signal(barrier, inc=1, device_id=(peer, col), device_id_type=MESH)
        return carry

    def greet_col(step, carry):
        peer = lax.rem(col + step, n_col)
        pl.semaphore_signal(barrier, inc=1, device_id=(row, peer), device_id_type=MESH)
        return carry

    loads = [
        pltpu.make_async_copy(source, target, in_sem.at[index])
        for index, (source, target) in enumerate(
            (
                (phase_hbm, phase),
                (trap_hbm, trap),
                (levels_hbm, levels),
                (old_hbm, old),
                (transfer_hbm, transfer),
            )
        )
    ]
    for load in loads:
        load.start()
    lax.fori_loop(1, n_row, greet_row, 0)
    lax.fori_loop(1, n_col, greet_col, 0)

    loads[0].wait()
    angle = phase[...]
    fields[row, :own, :] = jnp.cos(angle).astype(jnp.bfloat16)
    fields[row, own:, :] = jnp.sin(angle).astype(jnp.bfloat16)

    for load in loads[1:4]:
        load.wait()
    row_start = row * tile_rows
    strip = min(tile_rows, 128)

    def power_strip(index, carry):
        base = pl.multiple_of(index * strip, strip)
        pixel = lax.broadcasted_iota(jnp.int32, (strip, patterns), 0) + (row_start + base)

        def add_trap(k, total):
            where = jnp.broadcast_to(trap[pl.ds(k, 1), :], (strip, patterns))
            target = levels[pl.ds(k, 1), :].astype(jnp.float32)
            value = old[pl.ds(k, 1), :] * target * target
            value = jnp.broadcast_to(value, (strip, patterns))
            return total + jnp.where(pixel == where, value, 0.0)

        power[pl.ds(base, strip), :] = lax.fori_loop(
            0, traps, add_trap, jnp.zeros((strip, patterns), jnp.float32)
        )
        return carry

    lax.fori_loop(0, tile_rows // strip, power_strip, 0)

    pl.semaphore_wait(barrier, n_row + n_col - 2)

    def field_copy(peer, slot, step):
        return pltpu.make_async_remote_copy(
            src_ref=fields.at[slot],
            dst_ref=fields.at[slot],
            send_sem=field_send.at[step],
            recv_sem=field_recv.at[slot],
            device_id=(peer, col),
            device_id_type=MESH,
        )

    def send_field(step, carry):
        field_copy(lax.rem(row + step, n_row), row, step).start()
        return carry

    def take_field(step, carry):
        peer = lax.rem(row + n_row - step, n_row)
        field_copy(peer, peer, step).wait_recv()
        return carry

    lax.fori_loop(1, n_row, send_field, 0)
    loads[4].wait()
    lax.fori_loop(1, n_row, take_field, 0)

    field_re = fields[:, :own, :].reshape(patterns, phase.shape[1])
    field_im = fields[:, own:, :].reshape(patterns, phase.shape[1])
    with_real = jnp.concatenate([field_re, field_im], axis=0)
    with_imag = jnp.concatenate([-field_im, field_re], axis=0)
    over_modes = (((1,), (1,)), ((), ()))

    def rs_copy(peer, source, slot, step):
        return pltpu.make_async_remote_copy(
            src_ref=part.at[source],
            dst_ref=rs_buf.at[slot],
            send_sem=rs_send.at[step],
            recv_sem=rs_recv.at[slot],
            device_id=(row, peer),
            device_id_type=MESH,
        )

    my_chunk = col // group
    rows_per = group * pix_rows
    for turn in range(CHUNKS):
        chunk = lax.rem(my_chunk + turn + 1, CHUNKS)
        base = pl.multiple_of(chunk * rows_per, rows_per)
        first = lax.dot_general(
            transfer[0, pl.ds(base, rows_per), :], with_real, over_modes, preferred_element_type=jnp.float32
        )
        second = lax.dot_general(
            transfer[1, pl.ds(base, rows_per), :], with_imag, over_modes, preferred_element_type=jnp.float32
        )
        part[pl.ds(chunk * group, group)] = (
            (first + second).astype(jnp.bfloat16).reshape(group, pix_rows, 2 * patterns)
        )

        def send_part(index, carry):
            peer = chunk * group + lax.rem(index + col, group)

            @pl.when(peer != col)
            def _():
                rs_copy(peer, peer, col, peer).start()

            return carry

        lax.fori_loop(0, group, send_part, 0)

    def add_part(step, total):
        peer = lax.rem(col + n_col - step, n_col)
        rs_copy(peer, peer, peer, step).wait_recv()
        return total + rs_buf[peer].astype(jnp.float32)

    mine = lax.fori_loop(1, n_col, add_part, part[col].astype(jnp.float32)).astype(jnp.bfloat16)
    far_ref[...] = mine
    out_all[col] = mine

    def ag_copy(peer, slot, step):
        return pltpu.make_async_remote_copy(
            src_ref=out_all.at[slot],
            dst_ref=out_all.at[slot],
            send_sem=ag_send.at[step],
            recv_sem=ag_recv.at[slot],
            device_id=(row, peer),
            device_id_type=MESH,
        )

    def send_out(step, carry):
        ag_copy(lax.rem(col + step, n_col), col, step).start()
        return carry

    def take_out(step, carry):
        peer = lax.rem(col + n_col - step, n_col)
        ag_copy(peer, peer, step).wait_recv()
        return carry

    lax.fori_loop(1, n_col, send_out, 0)
    lax.fori_loop(1, n_col, take_out, 0)

    whole = out_all[...].reshape(tile_rows, 2 * patterns)
    out_re = whole[:, :patterns].astype(jnp.float32)
    out_im = whole[:, patterns:].astype(jnp.float32)
    square = out_re * out_re + out_im * out_im + 0.25
    amp_pix[...] = jnp.sqrt(square)
    gain = power[...] / square
    proj_re = (gain * out_re).astype(jnp.bfloat16).T
    proj_im = (gain * out_im).astype(jnp.bfloat16).T
    left_real = jnp.concatenate([proj_re, proj_im], axis=0)
    left_imag = jnp.concatenate([proj_im, -proj_re], axis=0)
    back = jnp.dot(left_real, transfer[0], preferred_element_type=jnp.float32) + jnp.dot(
        left_imag, transfer[1], preferred_element_type=jnp.float32
    )
    back = back.astype(jnp.bfloat16)
    stage[:, :own, :] = back[:patterns].reshape(n_row, own, back.shape[1])
    stage[:, own:, :] = back[patterns:].reshape(n_row, own, back.shape[1])

    def back_copy(peer, source, slot, step):
        return pltpu.make_async_remote_copy(
            src_ref=stage.at[source],
            dst_ref=back_buf.at[slot],
            send_sem=back_send.at[step],
            recv_sem=back_recv.at[slot],
            device_id=(peer, col),
            device_id_type=MESH,
        )

    def send_back(step, carry):
        peer = lax.rem(row + step, n_row)
        back_copy(peer, peer, row, step).start()
        return carry

    lax.fori_loop(1, n_row, send_back, 0)

    def find_trap(k, carry):
        where = jnp.broadcast_to(trap[pl.ds(k, 1), :], (tile_rows, patterns)) - row_start
        pixel = lax.broadcasted_iota(jnp.int32, (tile_rows, patterns), 0)
        found = jnp.where(pixel == where, amp_pix[...], 0.0)
        amp_rows[pl.ds(k, 1), :] = jnp.sum(found, axis=0, keepdims=True)
        return carry

    lax.fori_loop(0, traps, find_trap, 0)
    amp_buf[row] = amp_rows[...].astype(jnp.bfloat16)

    def amp_copy(peer, slot, step):
        return pltpu.make_async_remote_copy(
            src_ref=amp_buf.at[slot],
            dst_ref=amp_buf.at[slot],
            send_sem=amp_send.at[step],
            recv_sem=amp_recv.at[slot],
            device_id=(peer, col),
            device_id_type=MESH,
        )

    def send_amp(step, carry):
        amp_copy(lax.rem(row + step, n_row), row, step).start()
        return carry

    def add_back(step, total):
        peer = lax.rem(row + n_row - step, n_row)
        back_copy(peer, peer, peer, step).wait_recv()
        return total + back_buf[peer].astype(jnp.float32)

    def take_amp(step, carry):
        peer = lax.rem(row + n_row - step, n_row)
        amp_copy(peer, peer, step).wait_recv()
        return carry

    lax.fori_loop(1, n_row, send_amp, 0)
    total = lax.fori_loop(1, n_row, add_back, stage[row].astype(jnp.float32))
    lax.fori_loop(1, n_row, take_amp, 0)

    amp = jnp.sum(amp_buf[...].astype(jnp.float32), axis=0)
    ratio = amp / levels[...].astype(jnp.float32)
    mean = jnp.mean(ratio, axis=0, keepdims=True)
    weights_ref[...] = old[...] * mean / ratio
    lane = lax.broadcasted_iota(jnp.int32, (own, patterns), 1)
    place = lax.broadcasted_iota(jnp.int32, (own, patterns), 0) + row * own
    mine_mean = jnp.sum(
        jnp.where(lane == place, jnp.broadcast_to(mean, (own, patterns)), 0.0), axis=1, keepdims=True
    )
    factor = scale * mine_mean
    scaled_re = factor * total[:own]
    scaled_im = factor * total[own:]
    norm = jnp.sqrt(scaled_re * scaled_re + scaled_im * scaled_im + 1.0)
    slm_ref[0] = scaled_re / norm
    slm_ref[1] = scaled_im / norm

    def drain_row(step, carry):
        peer = lax.rem(row + step, n_row)
        field_copy(peer, row, step).wait_send()
        back_copy(peer, peer, row, step).wait_send()
        amp_copy(peer, row, step).wait_send()
        return carry

    def drain_col(step, carry):
        peer = lax.rem(col + step, n_col)
        rs_copy(peer, peer, col, peer).wait_send()
        ag_copy(peer, col, step).wait_send()
        return carry

    lax.fori_loop(1, n_row, drain_row, 0)
    lax.fori_loop(1, n_col, drain_col, 0)


def body(transfer, phase, trap_index, levels, weights_old):
    n_row = lax.axis_size("row")
    n_col = lax.axis_size("col")
    patterns, traps = trap_index.shape
    tile_rows, modes = transfer.shape[1:]
    pix_rows = tile_rows // n_col
    own = phase.shape[1]
    f32, bf16, i32 = jnp.float32, jnp.bfloat16, jnp.int32
    dma = pltpu.SemaphoreType.DMA
    far, weights, slm = pl.pallas_call(
        functools.partial(kernel, n_row, n_col, (MODES / TRAPS) ** 0.5),
        out_shape=(
            jax.ShapeDtypeStruct((pix_rows, 2 * patterns), bf16),
            jax.ShapeDtypeStruct((traps, patterns), f32),
            jax.ShapeDtypeStruct((2, own, modes), f32),
        ),
        in_specs=[pl.BlockSpec(memory_space=pl.ANY)] * 5,
        out_specs=[pl.BlockSpec(memory_space=pltpu.VMEM)] * 3,
        scratch_shapes=[
            pltpu.VMEM(transfer.shape, bf16),
            pltpu.VMEM((own, modes), f32),
            pltpu.VMEM((traps, patterns), i32),
            pltpu.VMEM((traps, patterns), i32),
            pltpu.VMEM((traps, patterns), f32),
            pltpu.VMEM((n_row, 2 * own, modes), bf16),
            pltpu.VMEM((n_col, pix_rows, 2 * patterns), bf16),
            pltpu.VMEM((n_col, pix_rows, 2 * patterns), bf16),
            pltpu.VMEM((n_col, pix_rows, 2 * patterns), bf16),
            pltpu.VMEM((tile_rows, patterns), f32),
            pltpu.VMEM((tile_rows, patterns), f32),
            pltpu.VMEM((n_row, 2 * own, modes), bf16),
            pltpu.VMEM((n_row, 2 * own, modes), bf16),
            pltpu.VMEM((traps, patterns), f32),
            pltpu.VMEM((n_row, traps, patterns), bf16),
            dma((5,)),
        ]
        + [dma((count,)) for count in (n_row, n_row, n_col, n_col, n_col, n_col, n_row, n_row, n_row, n_row)],
        compiler_params=pltpu.CompilerParams(
            collective_id=0, has_side_effects=True, vmem_limit_bytes=48 * 1024 * 1024
        ),
    )(transfer, phase.T, trap_index.T, levels.T, weights_old.T)
    return (far.reshape(pix_rows, 2, patterns), weights.T, slm.transpose(2, 0, 1))


def solution(mesh):
    placed = (P(None, "row", "col"), P("col", "row"), P(), P(), P())
    return jax.shard_map(
        body,
        mesh=mesh,
        in_specs=placed,
        out_specs=(P(("row", "col"), None, None), P(), P("col", None, "row")),
        check_vma=False,
    )
```

```python
import functools

import jax
import jax.numpy as jnp
from jax import lax
from jax.experimental import pallas as pl
from jax.experimental.pallas import tpu as pltpu
from jax.sharding import PartitionSpec as P

MODES = 16384
TRAPS = 64
MESH = pl.DeviceIdType.MESH
CHUNKS = 4


def kernel(
    n_row,
    n_col,
    scale,
    transfer_hbm,
    phase_hbm,
    trap_hbm,
    levels_hbm,
    old_hbm,
    far_ref,
    weights_ref,
    slm_ref,
    transfer,
    phase,
    trap,
    levels,
    old,
    fields,
    kept,
    pair_out,
    pair_in,
    part,
    rs_buf,
    out_all,
    power,
    amp_pix,
    stage,
    back_buf,
    half_out,
    half_in,
    amp_rows,
    amp_buf,
    amp_out,
    amp_in,
    in_sem,
    field_send,
    field_recv,
    pair_send,
    pair_recv,
    rs_send,
    rs_recv,
    ag_send,
    ag_recv,
    share_send,
    back_send,
    back_recv,
    amp_send,
    amp_recv,
    half_send,
    half_recv,
):
    row = lax.axis_index("row")
    col = lax.axis_index("col")
    core = lax.rem(col, 2)
    chip = col // 2
    n_chip = n_col // 2
    n_y = n_row // 2
    mate = col + 1 - 2 * core
    across = row + 1 - 2 * lax.rem(row, 2)
    pix_rows, patterns = rs_buf.shape[1], rs_buf.shape[2] // 2
    tile_rows = transfer.shape[1]
    own, modes = phase.shape
    traps = trap.shape[0]
    group = n_col // CHUNKS
    half = group // 2
    rows_per = group * pix_rows

    def along_y(step):
        return lax.rem(row + 2 * step, n_row)

    def before_y(step):
        return lax.rem(row + n_row - 2 * step, n_row)

    def chip_col(step):
        return 2 * lax.rem(chip + step, n_chip) + core

    def chip_before(step):
        return 2 * lax.rem(chip + n_chip - step, n_chip) + core

    def greet(device):
        pl.semaphore_signal(barrier, inc=1, device_id=device, device_id_type=MESH)

    barrier = pltpu.get_barrier_semaphore()
    greet((across, col))

    def greet_y(step, carry):
        greet((along_y(step), col))
        return carry

    def greet_chip(step, carry):
        greet((row, chip_col(step)))
        return carry

    lax.fori_loop(1, n_y, greet_y, 0)
    lax.fori_loop(1, n_chip, greet_chip, 0)
    greet((row, mate))

    loads = [
        pltpu.make_async_copy(source, target, in_sem.at[index])
        for index, (source, target) in enumerate(
            (
                (phase_hbm, phase),
                (trap_hbm, trap),
                (levels_hbm, levels),
                (old_hbm, old),
                (transfer_hbm, transfer),
            )
        )
    ]
    for load in loads:
        load.start()

    loads[0].wait()
    angle = phase[...]
    fields[row, :own, :] = jnp.cos(angle).astype(jnp.bfloat16)
    fields[row, own:, :] = jnp.sin(angle).astype(jnp.bfloat16)

    for load in loads[1:4]:
        load.wait()
    row_start = row * tile_rows
    strip = min(tile_rows, 128)

    def power_strip(index, carry):
        base = pl.multiple_of(index * strip, strip)
        pixel = lax.broadcasted_iota(jnp.int32, (strip, patterns), 0) + (row_start + base)

        def add_trap(k, total):
            where = jnp.broadcast_to(trap[pl.ds(k, 1), :], (strip, patterns))
            target = levels[pl.ds(k, 1), :].astype(jnp.float32)
            value = old[pl.ds(k, 1), :] * target * target
            value = jnp.broadcast_to(value, (strip, patterns))
            return total + jnp.where(pixel == where, value, 0.0)

        power[pl.ds(base, strip), :] = lax.fori_loop(
            0, traps, add_trap, jnp.zeros((strip, patterns), jnp.float32)
        )
        return carry

    lax.fori_loop(0, tile_rows // strip, power_strip, 0)
    pl.semaphore_wait(barrier, n_y + n_chip)

    def field_copy(peer, slot, step):
        return pltpu.make_async_remote_copy(
            src_ref=fields.at[slot],
            dst_ref=fields.at[slot],
            send_sem=field_send.at[step],
            recv_sem=field_recv.at[slot],
            device_id=(peer, col),
            device_id_type=MESH,
        )

    field_copy(across, row, 0).start()

    def send_own(step, carry):
        field_copy(along_y(step), row, step).start()
        return carry

    def send_across(step, carry):
        field_copy(along_y(step), across, n_y + step).start()
        return carry

    def take_field(step, carry):
        peer = before_y(step)
        field_copy(row, peer, step).wait_recv()
        return carry

    def take_across(step, carry):
        peer = lax.rem(across + n_row - 2 * step, n_row)
        field_copy(row, peer, step).wait_recv()
        return carry

    lax.fori_loop(1, n_y, send_own, 0)
    loads[4].wait()
    field_copy(across, across, 0).wait_recv()
    lax.fori_loop(1, n_y, send_across, 0)
    lax.fori_loop(1, n_y, take_field, 0)
    lax.fori_loop(1, n_y, take_across, 0)

    field_re = fields[:, :own, :].reshape(patterns, modes)
    field_im = fields[:, own:, :].reshape(patterns, modes)
    with_real = jnp.concatenate([field_re, field_im], axis=0)
    with_imag = jnp.concatenate([-field_im, field_re], axis=0)
    over_modes = (((1,), (1,)), ((), ()))

    def pair_copy(chunk):
        return pltpu.make_async_remote_copy(
            src_ref=pair_out.at[chunk],
            dst_ref=pair_in.at[chunk],
            send_sem=pair_send.at[chunk],
            recv_sem=pair_recv.at[chunk],
            device_id=(row, mate),
            device_id_type=MESH,
        )

    def rs_copy(peer, source, slot, step):
        return pltpu.make_async_remote_copy(
            src_ref=part.at[source],
            dst_ref=rs_buf.at[slot],
            send_sem=rs_send.at[step],
            recv_sem=rs_recv.at[slot],
            device_id=(row, peer),
            device_id_type=MESH,
        )

    my_chunk = col // group

    def order(turn):
        return lax.rem(my_chunk + turn + 1, CHUNKS)

    def make_chunk(chunk):
        base = pl.multiple_of(chunk * rows_per, rows_per)
        both = lax.dot_general(
            transfer[0, pl.ds(base, rows_per), :], with_real, over_modes, preferred_element_type=jnp.float32
        ) + lax.dot_general(
            transfer[1, pl.ds(base, rows_per), :], with_imag, over_modes, preferred_element_type=jnp.float32
        )
        both = both.reshape(half, 2, pix_rows, 2 * patterns)
        first = core == 0
        kept[chunk] = jnp.where(first, both[:, 0], both[:, 1])
        pair_out[chunk] = jnp.where(first, both[:, 1], both[:, 0]).astype(jnp.bfloat16)
        pair_copy(chunk).start()

    def send_chunk(chunk):
        pair_copy(chunk).wait_recv()
        total = kept[chunk] + pair_in[chunk].astype(jnp.float32)
        part[pl.ds(chunk * half, half)] = total.astype(jnp.bfloat16)

        def send_part(index, carry):
            target = chunk * half + lax.rem(index + chip, half)

            @pl.when(target != chip)
            def _():
                rs_copy(2 * target + core, target, chip, target).start()

            return carry

        lax.fori_loop(0, half, send_part, 0)

    make_chunk(order(0))
    for turn in range(1, CHUNKS):
        make_chunk(order(turn))
        send_chunk(order(turn - 1))
    send_chunk(order(CHUNKS - 1))

    def add_part(step, total):
        source = lax.rem(chip + n_chip - step, n_chip)
        rs_copy(col, source, source, 0).wait_recv()
        return total + rs_buf[source].astype(jnp.float32)

    mine = lax.fori_loop(1, n_chip, add_part, part[chip].astype(jnp.float32)).astype(jnp.bfloat16)
    far_ref[...] = mine
    out_all[col] = mine

    def ag_copy(peer, slot, step):
        return pltpu.make_async_remote_copy(
            src_ref=out_all.at[slot],
            dst_ref=out_all.at[slot],
            send_sem=ag_send.at[step],
            recv_sem=ag_recv.at[slot],
            device_id=(row, peer),
            device_id_type=MESH,
        )

    def share_copy(slot, step):
        return pltpu.make_async_remote_copy(
            src_ref=out_all.at[slot],
            dst_ref=out_all.at[slot],
            send_sem=share_send.at[step],
            recv_sem=ag_recv.at[slot],
            device_id=(row, mate),
            device_id_type=MESH,
        )

    def send_out(step, carry):
        ag_copy(chip_col(step), col, step).start()
        return carry

    def share_out(step, carry):
        slot = chip_before(step)
        ag_copy(col, slot, step).wait_recv()
        share_copy(slot, step).start()
        return carry

    def take_shared(step, carry):
        slot = chip_before(step) + 1 - 2 * core
        share_copy(slot, step).wait_recv()
        return carry

    lax.fori_loop(1, n_chip, send_out, 0)
    share_copy(col, 0).start()
    lax.fori_loop(1, n_chip, share_out, 0)
    lax.fori_loop(0, n_chip, take_shared, 0)

    whole = out_all[...].reshape(tile_rows, 2 * patterns)
    out_re = whole[:, :patterns].astype(jnp.float32)
    out_im = whole[:, patterns:].astype(jnp.float32)
    square = out_re * out_re + out_im * out_im + 0.25
    amp_pix[...] = jnp.sqrt(square).reshape(amp_pix.shape)
    gain = power[...] / square
    proj_re = (gain * out_re).astype(jnp.bfloat16).T
    proj_im = (gain * out_im).astype(jnp.bfloat16).T
    left_real = jnp.concatenate([proj_re, proj_im], axis=0)
    left_imag = jnp.concatenate([proj_im, -proj_re], axis=0)
    back = jnp.dot(left_real, transfer[0], preferred_element_type=jnp.float32) + jnp.dot(
        left_imag, transfer[1], preferred_element_type=jnp.float32
    )
    back = back.astype(jnp.bfloat16)
    stage[:, :own, :] = back[:patterns].reshape(n_row, own, modes)
    stage[:, own:, :] = back[patterns:].reshape(n_row, own, modes)

    def back_copy(peer, source, slot):
        return pltpu.make_async_remote_copy(
            src_ref=stage.at[source],
            dst_ref=back_buf.at[slot],
            send_sem=back_send.at[slot],
            recv_sem=back_recv.at[slot],
            device_id=(peer, col),
            device_id_type=MESH,
        )

    def send_far(step, carry):
        back_copy(along_y(step), lax.rem(across + 2 * step, n_row), n_y + step).start()
        return carry

    def send_near(step, carry):
        back_copy(along_y(step), along_y(step), step).start()
        return carry

    lax.fori_loop(1, n_y, send_far, 0)
    lax.fori_loop(1, n_y, send_near, 0)

    lanes = 8
    tiles = tile_rows // lanes

    def find_trap(k, carry):
        local = jnp.broadcast_to(trap[pl.ds(k, 1), :], (lanes, patterns)) - row_start
        width = tiles // 2
        upper = (local & (width * lanes)) != 0
        chosen = jnp.where(upper[None], amp_pix[pl.ds(width, width)], amp_pix[pl.ds(0, width)])
        while width > 1:
            width //= 2
            upper = (local & (width * lanes)) != 0
            chosen = jnp.where(upper[None], chosen[width:], chosen[:width])
        sub = lax.broadcasted_iota(jnp.int32, (lanes, patterns), 0)
        hit = ((local & (lanes - 1)) == sub) & (local >= 0) & (local < tile_rows)
        amp_rows[pl.ds(k, 1), :] = jnp.sum(jnp.where(hit, chosen[0], 0.0), axis=0, keepdims=True)
        return carry

    lax.fori_loop(0, traps, find_trap, 0, unroll=2)
    amp_out[0] = amp_rows[...].astype(jnp.bfloat16)

    def amp_copy(peer, slot):
        return pltpu.make_async_remote_copy(
            src_ref=amp_out.at[0],
            dst_ref=amp_buf.at[slot],
            send_sem=amp_send.at[slot],
            recv_sem=amp_recv.at[slot],
            device_id=(peer, col),
            device_id_type=MESH,
        )

    def send_amp(step, carry):
        amp_copy(along_y(step), step).start()
        return carry

    def add_far(step, total):
        back_copy(row, row, n_y + step).wait_recv()
        return total + back_buf[n_y + step].astype(jnp.float32)

    def add_near(step, total):
        back_copy(row, row, step).wait_recv()
        return total + back_buf[step].astype(jnp.float32)

    def add_amp(step, total):
        amp_copy(row, step).wait_recv()
        return total + amp_buf[step].astype(jnp.float32)

    lax.fori_loop(1, n_y, send_amp, 0)
    half_out[...] = lax.fori_loop(1, n_y, add_far, stage[across].astype(jnp.float32)).astype(jnp.bfloat16)
    half_copy = pltpu.make_async_remote_copy(
        src_ref=half_out,
        dst_ref=half_in,
        send_sem=half_send.at[0],
        recv_sem=half_recv.at[0],
        device_id=(across, col),
        device_id_type=MESH,
    )
    half_copy.start()
    amp_half = lax.fori_loop(1, n_y, add_amp, amp_out[0].astype(jnp.float32))
    amp_out[1] = amp_half.astype(jnp.bfloat16)
    amp_across = pltpu.make_async_remote_copy(
        src_ref=amp_out.at[1],
        dst_ref=amp_in,
        send_sem=half_send.at[1],
        recv_sem=half_recv.at[1],
        device_id=(across, col),
        device_id_type=MESH,
    )
    amp_across.start()
    near = lax.fori_loop(1, n_y, add_near, stage[row].astype(jnp.float32))
    half_copy.wait_recv()
    total = near + half_in[...].astype(jnp.float32)
    amp_across.wait_recv()

    amp = amp_half + amp_in[...].astype(jnp.float32)
    ratio = amp / levels[...].astype(jnp.float32)
    mean = jnp.mean(ratio, axis=0, keepdims=True)
    weights_ref[...] = old[...] * mean / ratio
    lane = lax.broadcasted_iota(jnp.int32, (own, patterns), 1)
    place = lax.broadcasted_iota(jnp.int32, (own, patterns), 0) + row * own
    mine_mean = jnp.sum(
        jnp.where(lane == place, jnp.broadcast_to(mean, (own, patterns)), 0.0), axis=1, keepdims=True
    )
    factor = scale * mine_mean
    scaled_re = factor * total[:own]
    scaled_im = factor * total[own:]
    norm = jnp.sqrt(scaled_re * scaled_re + scaled_im * scaled_im + 1.0)
    slm_ref[0] = scaled_re / norm
    slm_ref[1] = scaled_im / norm

    def drain_y(step, carry):
        field_copy(row, row, step).wait_send()
        field_copy(row, row, n_y + step).wait_send()
        back_copy(row, row, step).wait_send()
        back_copy(row, row, n_y + step).wait_send()
        amp_copy(row, step).wait_send()
        return carry

    def drain_chip(step, carry):
        target = lax.rem(chip + step, n_chip)
        rs_copy(col, target, chip, target).wait_send()
        ag_copy(col, col, step).wait_send()
        share_copy(col, step).wait_send()
        return carry

    field_copy(across, row, 0).wait_send()
    share_copy(col, 0).wait_send()
    for chunk in range(CHUNKS):
        pair_copy(chunk).wait_send()
    lax.fori_loop(1, n_y, drain_y, 0)
    lax.fori_loop(1, n_chip, drain_chip, 0)
    half_copy.wait_send()
    amp_across.wait_send()


def body(transfer, phase, trap_index, levels, weights_old):
    n_row = lax.axis_size("row")
    n_col = lax.axis_size("col")
    patterns, traps = trap_index.shape
    tile_rows, modes = transfer.shape[1:]
    pix_rows = tile_rows // n_col
    own = phase.shape[1]
    n_y, n_chip = n_row // 2, n_col // 2
    half = n_chip // CHUNKS
    f32, bf16, i32 = jnp.float32, jnp.bfloat16, jnp.int32
    dma = pltpu.SemaphoreType.DMA
    arrays = (transfer, phase.T, trap_index.T, levels.T, weights_old.T)
    block = (pix_rows, 2 * patterns)
    far, weights, slm = pl.pallas_call(
        functools.partial(kernel, n_row, n_col, (MODES / TRAPS) ** 0.5),
        out_shape=(
            jax.ShapeDtypeStruct(block, bf16),
            jax.ShapeDtypeStruct((traps, patterns), f32),
            jax.ShapeDtypeStruct((2, own, modes), f32),
        ),
        in_specs=[pl.BlockSpec(memory_space=pl.ANY)] * 5,
        out_specs=[pl.BlockSpec(memory_space=pltpu.VMEM)] * 3,
        scratch_shapes=[
            pltpu.VMEM(transfer.shape, bf16),
            pltpu.VMEM((own, modes), f32),
            pltpu.VMEM((traps, patterns), i32),
            pltpu.VMEM((traps, patterns), i32),
            pltpu.VMEM((traps, patterns), f32),
            pltpu.VMEM((n_row, 2 * own, modes), bf16),
            pltpu.VMEM((CHUNKS, half) + block, f32),
            pltpu.VMEM((CHUNKS, half) + block, bf16),
            pltpu.VMEM((CHUNKS, half) + block, bf16),
            pltpu.VMEM((n_chip,) + block, bf16),
            pltpu.VMEM((n_chip,) + block, bf16),
            pltpu.VMEM((n_col,) + block, bf16),
            pltpu.VMEM((tile_rows, patterns), f32),
            pltpu.VMEM((tile_rows // 8, 8, patterns), f32),
            pltpu.VMEM((n_row, 2 * own, modes), bf16),
            pltpu.VMEM((n_row, 2 * own, modes), bf16),
            pltpu.VMEM((2 * own, modes), bf16),
            pltpu.VMEM((2 * own, modes), bf16),
            pltpu.VMEM((traps, patterns), f32),
            pltpu.VMEM((n_y, traps, patterns), bf16),
            pltpu.VMEM((2, traps, patterns), bf16),
            pltpu.VMEM((traps, patterns), bf16),
        ]
        + [
            dma((count,))
            for count in (5, n_row, n_row, CHUNKS, CHUNKS, n_chip, n_chip, n_chip, n_col, n_chip)
            + (n_row, n_row, n_y, n_y, 2, 2)
        ],
        compiler_params=pltpu.CompilerParams(
            collective_id=0, has_side_effects=True, vmem_limit_bytes=48 * 1024 * 1024
        ),
    )(*(pltpu.with_memory_space_constraint(array, pltpu.HBM) for array in arrays))
    return (far.reshape(pix_rows, 2, patterns), weights.T, slm.transpose(2, 0, 1))


def solution(mesh):
    placed = (P(None, "row", "col"), P("col", "row"), P(), P(), P())
    return jax.shard_map(
        body,
        mesh=mesh,
        in_specs=placed,
        out_specs=(P(("row", "col"), None, None), P(), P("col", None, "row")),
        check_vma=False,
    )
```
